512 devices in a mesh: row: 32 (over x, z_hi, core), col: 16 (over z_lo, y).
Axes of the slice: x: 4, y: 4, z: 16 (z_hi: 4, z_lo: 4; z = z_hi * 4 + z_lo), core: 2. Of those that a mesh axis runs over, the one named last changes fastest.
Arguments:
- top_inverse: float32 [2, 4096, 4096], P(None, 'row', 'col'), may hold values from -6 to 6
- panel: float32 [2, 2048, 8192], P(None, 'row', 'col'), may hold values from -0.09375 to 0.09375
- leaf_rows: int32 [32, 8], P('col'), may hold values from 0 to 15, as said below
- leaf_counts: int32 [32], P('col'), may hold values from 1 to 8, as said below
- diag_inverse: float32 [2, 256, 8192], P(None, 'row', 'col'), may hold values from -6 to 6
Outputs:
- selected: float32 [2, 4096, 8192], P(None, 'row', 'col')
- diagonal: float32 [2, 256, 8192], P(None, 'row', 'col')
The draws below stay inside these ranges and needn't reach their ends.
Inputs may be any that keep to these rules, and one draw needn't show every extreme that they name: `leaf_rows`: the 8 entries of each leaf are distinct separator blocks. Slots 0 to leaf_counts - 1 of a leaf are live.
All inputs are finite; a program needn't handle non-finite values.
Results may differ from the reference program's by a relative error of at most 0.0003.
Values sent between devices are 32-bit elements; how exact they have to be, the bound alone decides.
A program may use at most 128 MiB of HBM per device.

```python
import jax
import jax.numpy as jnp
from jax import lax

B = 256
NT = 16
P_SIZE = 8
NLEAF = 32


def draw_leaf_rows(key, part):
    leaf_keys = jax.random.split(key, NLEAF)
    shuffled = jax.vmap(lambda leaf_key: jax.random.permutation(leaf_key, NT))(leaf_keys)
    return shuffled[:, :P_SIZE].astype(jnp.int32)


def draw_leaf_counts(key, part):
    first_key, second_key, third_key = jax.random.split(jax.random.fold_in(key, 7), 3)
    live_counts = jax.random.randint(first_key, (NLEAF,), 1, P_SIZE + 1)
    full_leaf = jax.random.randint(second_key, (), 0, NLEAF)
    short_leaf = (full_leaf + 1 + jax.random.randint(third_key, (), 0, NLEAF - 1)) % NLEAF
    return live_counts.at[full_leaf].set(P_SIZE).at[short_leaf].set(1).astype(jnp.int32)


def level_of(own_key, extent, cuts, smallest, largest):
    loudness, own = 1.0, jax.random.fold_in(own_key, 6)
    for dim, shards_of in cuts:
        heights = jnp.exp(jax.random.uniform(jax.random.fold_in(own, dim), (shards_of,), jnp.float32, smallest / len(cuts), largest / len(cuts)))
        loudness = loudness * jnp.repeat(heights, extent[dim] // shards_of).reshape([-1 if axis == dim else 1 for axis in range(len(extent))])
    return loudness


def gaussian(own_key, shape, width, reach, cuts=(), held_as=jnp.bfloat16):
    entries = jax.random.normal(own_key, shape, jnp.float32) * width
    if len(cuts) > 0:
        entries = level_of(own_key, shape, cuts, -0.22, 0.18) * entries
    return jnp.clip(entries, min=-reach, max=reach).astype(held_as)


def setup_inputs(seed: int = 0) -> dict:
    seeds = jax.random.split(jax.random.key(seed), 6)
    return {
        "top_inverse": gaussian(seeds[0], (2, NT * B, NT * B), 1.0, 6.0, ((1, 32), (2, 16)), jnp.float32),
        "panel": gaussian(seeds[1], (2, P_SIZE * B, NLEAF * B), (2 * P_SIZE * B) ** -0.5, 0.09375, ((1, 32), (2, 16)), jnp.float32),
        "leaf_rows": draw_leaf_rows(jax.random.fold_in(seeds[5], 71), 0),
        "leaf_counts": draw_leaf_counts(jax.random.fold_in(seeds[5], 71), 0),
        "diag_inverse": gaussian(seeds[4], (2, B, NLEAF * B), 0.5, 6.0, ((1, 32), (2, 16)), jnp.float32),
    }


def complex_product(left_real, left_imag, right_real, right_imag):
    def product_highest(left, right):
        return jnp.dot(left, right, precision=lax.Precision.HIGHEST, preferred_element_type=jnp.float32)
    real_part = product_highest(left_real, right_real) - product_highest(left_imag, right_imag)
    imag_part = product_highest(left_real, right_imag) + product_highest(left_imag, right_real)
    return real_part, imag_part


def reference(top_inverse, panel, leaf_rows, leaf_counts, diag_inverse):
    inner = jnp.arange(B, dtype=jnp.int32)

    def one_leaf(member):
        rows_here = lax.dynamic_index_in_dim(leaf_rows, member, 0, keepdims=False)
        live_count = lax.dynamic_index_in_dim(leaf_counts, member, 0, keepdims=False)
        gather_index = (rows_here[:, None] * B + inner[None, :]).reshape(-1).astype(jnp.int32)
        active = ((jnp.arange(P_SIZE * B, dtype=jnp.int32) // B) < live_count).astype(jnp.float32)
        submatrix = jnp.take(jnp.take(top_inverse, gather_index, axis=1), gather_index, axis=2)
        lower = lax.dynamic_slice_in_dim(panel, member * B, B, 2) * active[None, :, None]
        real_part, imag_part = complex_product(submatrix[0], submatrix[1], lower[0], lower[1])
        sel_real = -real_part * active[:, None]
        sel_imag = -imag_part * active[:, None]
        diag_real, diag_imag = complex_product(sel_real.T, sel_imag.T, lower[0], lower[1])
        diag_block = lax.dynamic_slice_in_dim(diag_inverse, member * B, B, 2)
        return (jnp.stack([sel_real, sel_imag]), jnp.stack([diag_block[0] - diag_real, diag_block[1] - diag_imag]), gather_index)

    blocks, diagonal, indices = lax.map(one_leaf, jnp.arange(NLEAF, dtype=jnp.int32))
    dense = jnp.zeros((2, NT * B, NLEAF, B), jnp.float32)
    leaf_ids = jnp.arange(NLEAF, dtype=jnp.int32)[:, None]
    dense = dense.at[:, indices, leaf_ids, :].set(jnp.transpose(blocks, (1, 0, 2, 3)))
    selected = dense.reshape(2, NT * B, NLEAF * B)
    diagonal = jnp.transpose(diagonal, (1, 2, 0, 3)).reshape(2, B, NLEAF * B)
    return selected, diagonal
```

```python
import jax
import jax.numpy as jnp
from jax import lax
from jax.experimental import pallas as pl
from jax.experimental.pallas import tpu as pltpu
from jax.sharding import PartitionSpec as P

MESH = pl.DeviceIdType.MESH
B = 256
SLOTS = 8
LEAVES = 2
RING = 4


def split(value):
    high = value.astype(jnp.bfloat16)
    low = (value - high.astype(jnp.float32)).astype(jnp.bfloat16)
    return high, low


def dot(left, right):
    return jnp.dot(left, right, preferred_element_type=jnp.float32)


def dot_t(left, right):
    return lax.dot_general(
        left, right, (((0,), (0,)), ((), ())), preferred_element_type=jnp.float32
    )


def kernel(
    rows_ref,
    counts_ref,
    top_ref,
    panel_ref,
    diag_ref,
    sel_ref,
    out_ref,
    a_buf,
    l_buf0,
    l_buf1,
    acc,
    d_buf,
    sib_buf,
    c_buf,
    x1_buf,
    x2_buf,
    e_buf,
    z1_buf,
    z2_buf,
    local_sem,
    az_own,
    az_fwd,
    az_recv,
    ay_send,
    ay_recv,
    lz_send,
    lz_recv,
    lx_send,
    lx_recv,
    lc_send,
    lc_recv,
    rs_send,
    rs_recv,
):
    l_buf = (l_buf0, l_buf1)
    row = lax.axis_index("row")
    col = lax.axis_index("col")
    x, zh, c = row // 8, (row // 2) % 4, row % 2
    zl, y = col // 4, col % 4

    def mod4(v):
        return (v + 8) % 4

    def row_of(xx, zz, cc):
        return (mod4(xx) * 4 + mod4(zz)) * 2 + cc

    sib = (row_of(x, zh, 1 - c), col)
    x_dev = {d: (row_of(x + d, zh, c), col) for d in (-1, 1)}
    zh_dev = {d: (row_of(x, zh + d, c), col) for d in (-1, 1)}
    y_dev = {d: (row, zl * 4 + mod4(y + d)) for d in (-1, 1)}

    own = [
        pltpu.make_async_copy(top_ref, a_buf.at[col], local_sem.at[0]),
    ] + [
        pltpu.make_async_copy(
            panel_ref.at[:, :, pl.ds(m * B, B)], l_buf[m].at[row], local_sem.at[1 + m]
        )
        for m in range(LEAVES)
    ]
    for copy in own:
        copy.start()

    barrier = pltpu.get_barrier_semaphore()
    greet = [sib, x_dev[-1], x_dev[1], zh_dev[-1], zh_dev[1], y_dev[-1], y_dev[1]]
    greet += [(row, mod4(zl + d) * 4 + y) for d in (-1, 1)]
    for dev in greet:
        pl.semaphore_signal(barrier, inc=1, device_id=dev, device_id_type=MESH)
    pl.semaphore_wait(barrier, len(greet))
    for copy in own:
        copy.wait()

    sent = []

    def desc(src, dst, ss, rs, dev):
        return pltpu.make_async_remote_copy(
            src_ref=src,
            dst_ref=dst,
            send_sem=ss,
            recv_sem=rs,
            device_id=dev,
            device_id_type=MESH,
        )

    def send(src, dst, ss, rs, dev):
        copy = desc(src, dst, ss, rs, dev)
        copy.start()
        sent.append(copy)

    def arrive(dst, ss, rs):
        desc(dst, dst, ss, rs, sib).wait_recv()

    def a_block(b, yy):
        return a_buf.at[b * 4 + mod4(yy)]

    def a_y_start(b):
        for t, d in enumerate((1, -1)):
            ref = a_block(b, y)
            send(ref, ref, ay_send.at[b, t], ay_recv.at[b, t], y_dev[d])

    def a_y_forward(b):
        for t, d in enumerate((1, -1)):
            ref = a_block(b, y - d)
            arrive(ref, ay_send.at[b, t], ay_recv.at[b, t])
            half = ref.at[t]
            send(half, half, ay_send.at[b, 2 + t], ay_recv.at[b, 2 + t], y_dev[d])

    def a_y_finish(b):
        for t in range(2):
            half = a_block(b, y + 2).at[t]
            arrive(half, ay_send.at[b, 2 + t], ay_recv.at[b, 2 + t])

    conditional = []

    def a_z_send(cond, b, dev_zl, ss):
        ref = a_block(b, y)
        copy = desc(ref, ref, ss, az_recv.at[b], (row, dev_zl * 4 + y))
        pl.when(cond)(copy.start)
        conditional.append((cond, copy))

    other = [
        jnp.where(zl == 0, 1, jnp.where(zl == 1, 0, jnp.where(zl == 2, 1, 2))),
        jnp.where(zl == 0, 2, jnp.where(zl == 1, 2, jnp.where(zl == 2, 3, 1))),
        jnp.where(zl == 0, 3, jnp.where(zl == 1, 3, 0)),
    ]

    def a_z_step(i):
        b = other[i]
        arrive(a_block(b, y), az_fwd.at[b], az_recv.at[b])
        from_left = b < zl
        dev_zl = jnp.where(from_left, zl + 1, zl - 1)
        a_z_send((dev_zl >= 0) & (dev_zl <= 3), b, mod4(dev_zl), az_fwd.at[b])
        a_y_start(b)

    offsets = (0, -1, 1, 2)

    def l_block(m, k, dx):
        return l_buf[m].at[row_of(x + dx, zh + offsets[k], c)]

    def l_sib_block(m, k, dx):
        return l_buf[m].at[row_of(x + dx, zh + offsets[k], 1 - c)]

    def l_relay(m, k, t):
        ref = l_block(m, k, offsets[t])
        send(ref, ref, lc_send.at[m, k, t], lc_recv.at[m, k, t], sib)

    def l_z_start(m):
        ref = l_block(m, 0, 0)
        for t, d in enumerate((1, -1)):
            send(ref, ref, lz_send.at[m, t], lz_recv.at[m, t], zh_dev[d])

    def l_z_forward(m):
        for t, d in enumerate((1, -1)):
            ref = l_block(m, 1 + t, 0)
            arrive(ref, lz_send.at[m, t], lz_recv.at[m, t])
            half = ref.at[t]
            send(half, half, lz_send.at[m, 2 + t], lz_recv.at[m, 2 + t], zh_dev[d])
            l_x_start(m, 1 + t)

    def l_z_finish(m):
        for t in range(2):
            half = l_block(m, 3, 0).at[t]
            arrive(half, lz_send.at[m, 2 + t], lz_recv.at[m, 2 + t])
        l_x_start(m, 3)

    def l_x_start(m, k):
        ref = l_block(m, k, 0)
        for t, d in enumerate((1, -1)):
            send(ref, ref, lx_send.at[m, k, t], lx_recv.at[m, k, t], x_dev[d])
        l_relay(m, k, 0)

    def l_x_forward(m, k):
        for t, d in enumerate((1, -1)):
            ref = l_block(m, k, -d)
            arrive(ref, lx_send.at[m, k, t], lx_recv.at[m, k, t])
            half = ref.at[t]
            send(half, half, lx_send.at[m, k, 2 + t], lx_recv.at[m, k, 2 + t], x_dev[d])
            l_relay(m, k, 1 + t)

    def l_x_finish(m, k):
        for t in range(2):
            half = l_block(m, k, 2).at[t]
            arrive(half, lx_send.at[m, k, 2 + t], lx_recv.at[m, k, 2 + t])
        l_relay(m, k, 3)

    def l_sib_finish(m):
        for k in range(4):
            for t in range(4):
                arrive(l_sib_block(m, k, offsets[t]), lc_send.at[m, k, t], lc_recv.at[m, k, t])

    block_row = row // 2

    def leaf_state(m):
        count = counts_ref[m]
        place, live = jnp.int32(0), jnp.int32(0)
        for q in range(SLOTS):
            hit = ((rows_ref[m, q] == block_row) & (count > q)).astype(jnp.int32)
            place += hit * q
            live += hit
        return count, place, live

    def compute(m):
        count, place, live = leaf_state(m)
        acc[...] = jnp.zeros_like(acc)

        def step(q, carry):
            active = (count > q).astype(jnp.int32).astype(jnp.float32)
            left = a_buf[rows_ref[m, q]].reshape(B, B)
            a_high, a_low = split(left)
            for part in range(2):
                right = l_buf[m][pl.ds(q * 4, 4), part].reshape(B, B) * active
                r_high, r_low = split(right)
                acc[part] += dot(a_high, r_high) + (dot(a_low, r_high) + dot(a_high, r_low))
            return carry

        lax.fori_loop(0, SLOTS, step, 0)
        keep = -(live.astype(jnp.float32))
        half = B // 2
        real = (acc[0, :half] - acc[1, half:]) * keep
        imag = (acc[1, :half] + acc[0, half:]) * keep
        sel_ref[0, :, pl.ds(m * B, B)] = real
        sel_ref[1, :, pl.ds(m * B, B)] = imag

    def diagonal(m):
        count, place, live = leaf_state(m)
        half = B // 2
        real = sel_ref[0, :, pl.ds(m * B, B)]
        imag = sel_ref[1, :, pl.ds(m * B, B)]
        low = l_buf[m][pl.ds(place * 4 + c * 2, 2)]
        low_real, low_imag = low[:, 0].reshape(half, B), low[:, 1].reshape(half, B)
        for part in range(2):
            if part == 0:
                left = jnp.concatenate([real, -imag], axis=0)
                right = jnp.concatenate([low_real, low_imag], axis=0)
            else:
                left = jnp.concatenate([real, imag], axis=0)
                right = jnp.concatenate([low_imag, low_real], axis=0)
            l_high, l_low = split(left)
            r_high, r_low = split(right)
            value = dot_t(l_high, r_high) + (dot_t(l_low, r_high) + dot_t(l_high, r_low))
            d_buf[m, :, :, part] = value.reshape(16, 2, 8, B)

    def rs0(m):
        send(d_buf.at[m, :, 1 - c], sib_buf.at[m], rs_send.at[m, 0], rs_recv.at[m, 0], sib)

    def rs1(m):
        arrive(sib_buf.at[m], rs_send.at[m, 0], rs_recv.at[m, 0])
        c_buf[m] = (d_buf[m, :, c] + sib_buf[m]).reshape(4, 4, 2, 8, B)
        for t, d in enumerate((1, -1)):
            send(
                c_buf.at[m, mod4(x + 2), :, t],
                x1_buf.at[m, t],
                rs_send.at[m, 1 + t],
                rs_recv.at[m, 1 + t],
                x_dev[d],
            )

    def rs2(m):
        for t, d in enumerate((1, -1)):
            arrive(x1_buf.at[m, t], rs_send.at[m, 1 + t], rs_recv.at[m, 1 + t])
            place = mod4(x + d)
            c_buf[m, place, :, t] = c_buf[m, place, :, t] + x1_buf[m, t]
            send(
                c_buf.at[m, place],
                x2_buf.at[m, t],
                rs_send.at[m, 3 + t],
                rs_recv.at[m, 3 + t],
                x_dev[d],
            )

    def rs3(m):
        for t in range(2):
            arrive(x2_buf.at[m, t], rs_send.at[m, 3 + t], rs_recv.at[m, 3 + t])
        e_buf[m] = c_buf[m, x] + (x2_buf[m, 0] + x2_buf[m, 1])
        for t, d in enumerate((1, -1)):
            send(
                e_buf.at[m, mod4(zh + 2), t],
                z1_buf.at[m, t],
                rs_send.at[m, 5 + t],
                rs_recv.at[m, 5 + t],
                zh_dev[d],
            )

    def rs4(m):
        for t, d in enumerate((1, -1)):
            arrive(z1_buf.at[m, t], rs_send.at[m, 5 + t], rs_recv.at[m, 5 + t])
            place = mod4(zh + d)
            e_buf[m, place, t] = e_buf[m, place, t] + z1_buf[m, t]
            send(
                e_buf.at[m, place],
                z2_buf.at[m, t],
                rs_send.at[m, 7 + t],
                rs_recv.at[m, 7 + t],
                zh_dev[d],
            )

    def rs5(m):
        for t in range(2):
            arrive(z2_buf.at[m, t], rs_send.at[m, 7 + t], rs_recv.at[m, 7 + t])
        total = e_buf[m, zh] + (z2_buf[m, 0] + z2_buf[m, 1])
        out_ref[:, :, pl.ds(m * B, B)] = diag_ref[:, :, pl.ds(m * B, B)] - total

    a_z_send(zl < 3, zl, mod4(zl + 1), az_own.at[0])
    a_z_send(zl > 0, zl, mod4(zl - 1), az_own.at[1])
    a_y_start(zl)
    l_z_start(0)
    l_x_start(0, 0)
    l_x_start(1, 0)
    a_z_step(0)
    a_y_forward(zl)
    l_x_forward(0, 0)
    l_x_forward(1, 0)
    l_x_finish(0, 0)
    l_x_finish(1, 0)
    a_z_step(1)
    l_z_forward(0)
    l_z_start(1)
    a_y_forward(other[0])
    a_y_finish(zl)
    l_x_forward(0, 1)
    l_x_forward(0, 2)
    a_z_step(2)
    a_y_forward(other[1])
    a_y_finish(other[0])
    l_z_finish(0)
    l_x_finish(0, 1)
    l_x_finish(0, 2)
    l_z_forward(1)
    a_y_forward(other[2])
    a_y_finish(other[1])
    l_x_forward(0, 3)
    l_x_forward(1, 1)
    l_x_forward(1, 2)
    a_y_finish(other[2])
    l_x_finish(0, 3)
    l_x_finish(1, 1)
    l_x_finish(1, 2)
    l_sib_finish(0)
    compute(0)
    diagonal(0)
    rs0(0)
    l_z_finish(1)
    l_x_forward(1, 3)
    rs1(0)
    l_x_finish(1, 3)
    l_sib_finish(1)
    compute(1)
    diagonal(1)
    rs0(1)
    rs2(0)
    rs1(1)
    rs3(0)
    rs2(1)
    rs4(0)
    rs3(1)
    rs5(0)
    rs4(1)
    rs5(1)
    for copy in sent:
        copy.wait_send()
    for cond, copy in conditional:
        pl.when(cond)(copy.wait_send)


def on_device(top_inverse, panel, leaf_rows, leaf_counts, diag_inverse):
    f32 = jnp.float32
    any_space = pl.BlockSpec(memory_space=pl.ANY)
    vmem = pl.BlockSpec(memory_space=pltpu.VMEM)
    smem = pl.BlockSpec(memory_space=pltpu.SMEM)
    dma = pltpu.SemaphoreType.DMA
    return pl.pallas_call(
        kernel,
        out_shape=(
            jax.ShapeDtypeStruct((2, B // 2, LEAVES * B), f32),
            jax.ShapeDtypeStruct((2, 8, LEAVES * B), f32),
        ),
        in_specs=[smem, smem, any_space, any_space, vmem],
        out_specs=(vmem, vmem),
        scratch_shapes=[
            pltpu.VMEM((16, 2, B // 2, B), f32),
            pltpu.VMEM((32, 2, 64, B), f32),
            pltpu.VMEM((32, 2, 64, B), f32),
            pltpu.VMEM((2, B, B), f32),
            pltpu.VMEM((LEAVES, 16, 2, 2, 8, B), f32),
            pltpu.VMEM((LEAVES, 16, 2, 8, B), f32),
            pltpu.VMEM((LEAVES, 4, 4, 2, 8, B), f32),
            pltpu.VMEM((LEAVES, 2, 4, 8, B), f32),
            pltpu.VMEM((LEAVES, 2, 4, 2, 8, B), f32),
            pltpu.VMEM((LEAVES, 4, 2, 8, B), f32),
            pltpu.VMEM((LEAVES, 2, 8, B), f32),
            pltpu.VMEM((LEAVES, 2, 2, 8, B), f32),
            dma((3,)),
            dma((2,)),
            dma((4,)),
            dma((4,)),
            dma((4, 4)),
            dma((4, 4)),
            dma((LEAVES, 4)),
            dma((LEAVES, 4)),
            dma((LEAVES, 4, 4)),
            dma((LEAVES, 4, 4)),
            dma((LEAVES, 4, 4)),
            dma((LEAVES, 4, 4)),
            dma((LEAVES, 9)),
            dma((LEAVES, 9)),
        ],
        compiler_params=pltpu.CompilerParams(collective_id=0, has_side_effects=True),
    )(leaf_rows, leaf_counts, top_inverse, panel, diag_inverse)


def solution(mesh):
    return jax.shard_map(
        on_device,
        mesh=mesh,
        in_specs=(
            P(None, "row", "col"),
            P(None, "row", "col"),
            P("col", None),
            P("col"),
            P(None, "row", "col"),
        ),
        out_specs=(P(None, "row", "col"), P(None, "row", "col")),
        check_vma=False,
    )
```

```python
import jax
import jax.numpy as jnp
from jax import lax
from jax.experimental import pallas as pl
from jax.experimental.pallas import tpu as pltpu
from jax.sharding import PartitionSpec as P

MESH = pl.DeviceIdType.MESH
B = 256
SLOTS = 8
LEAVES = 2
CHUNKS = ((0, 0, 256), (1, 0, 128), (1, 128, 128))
NC = len(CHUNKS)


def split(value):
    high = value.astype(jnp.bfloat16)
    low = (value - high.astype(jnp.float32)).astype(jnp.bfloat16)
    return high, low


def dot(left, right):
    return jnp.dot(left, right, preferred_element_type=jnp.float32)


def dot_t(left, right):
    return lax.dot_general(
        left, right, (((0,), (0,)), ((), ())), preferred_element_type=jnp.float32
    )


def kernel(
    rows_ref,
    counts_ref,
    top_ref,
    panel_ref,
    diag_ref,
    sel_ref,
    out_ref,
    a_buf,
    l_buf0,
    l_buf1,
    a_hl,
    acc,
    d_buf,
    sib_buf,
    c_buf,
    x1_buf,
    x2_buf,
    e_buf,
    z1_buf,
    z2_buf,
    local_sem,
    az_own,
    az_fwd,
    az_recv,
    ay_send,
    ay_recv,
    lz_send,
    lz_recv,
    lx_send,
    lx_recv,
    lc_send,
    lc_recv,
    rs_send,
    rs_recv,
):
    l_buf = (l_buf0, l_buf1)
    row = lax.axis_index("row")
    col = lax.axis_index("col")
    x, zh, c = row // 8, (row // 2) % 4, row % 2
    zl, y = col // 4, col % 4

    def mod4(v):
        return (v + 8) % 4

    def row_of(xx, zz, cc):
        return (mod4(xx) * 4 + mod4(zz)) * 2 + cc

    sib = (row_of(x, zh, 1 - c), col)
    x_dev = {d: (row_of(x + d, zh, c), col) for d in (-1, 1)}
    zh_dev = {d: (row_of(x, zh + d, c), col) for d in (-1, 1)}
    y_dev = {d: (row, zl * 4 + mod4(y + d)) for d in (-1, 1)}

    own = [
        pltpu.make_async_copy(top_ref, a_buf.at[col], local_sem.at[0]),
    ] + [
        pltpu.make_async_copy(
            panel_ref.at[:, :, pl.ds(m * B, B)], l_buf[m].at[row], local_sem.at[1 + m]
        )
        for m in range(LEAVES)
    ]
    for copy in own:
        copy.start()

    barrier = pltpu.get_barrier_semaphore()
    greet = [sib, x_dev[-1], x_dev[1], zh_dev[-1], zh_dev[1], y_dev[-1], y_dev[1]]
    greet += [(row, mod4(zl + d) * 4 + y) for d in (-1, 1)]
    for dev in greet:
        pl.semaphore_signal(barrier, inc=1, device_id=dev, device_id_type=MESH)
    pl.semaphore_wait(barrier, len(greet))
    for copy in own:
        copy.wait()

    sent = []

    def desc(src, dst, ss, rs, dev):
        return pltpu.make_async_remote_copy(
            src_ref=src,
            dst_ref=dst,
            send_sem=ss,
            recv_sem=rs,
            device_id=dev,
            device_id_type=MESH,
        )

    def send(src, dst, ss, rs, dev):
        copy = desc(src, dst, ss, rs, dev)
        copy.start()
        sent.append(copy)

    def arrive(dst, ss, rs):
        desc(dst, dst, ss, rs, sib).wait_recv()

    def a_block(b, yy):
        return a_buf.at[b * 4 + mod4(yy)]

    def a_y_start(b):
        for t, d in enumerate((1, -1)):
            ref = a_block(b, y)
            send(ref, ref, ay_send.at[b, t], ay_recv.at[b, t], y_dev[d])

    def a_y_forward(b):
        for t, d in enumerate((1, -1)):
            ref = a_block(b, y - d)
            arrive(ref, ay_send.at[b, t], ay_recv.at[b, t])
            half = ref.at[t]
            send(half, half, ay_send.at[b, 2 + t], ay_recv.at[b, 2 + t], y_dev[d])

    def a_y_forward1(b, t):
        d = (1, -1)[t]
        ref = a_block(b, y - d)
        arrive(ref, ay_send.at[b, t], ay_recv.at[b, t])
        half = ref.at[t]
        send(half, half, ay_send.at[b, 2 + t], ay_recv.at[b, 2 + t], y_dev[d])

    def a_y_finish(b):
        for t in range(2):
            half = a_block(b, y + 2).at[t]
            arrive(half, ay_send.at[b, 2 + t], ay_recv.at[b, 2 + t])

    conditional = []

    def a_z_send(cond, b, dev_zl, ss):
        ref = a_block(b, y)
        copy = desc(ref, ref, ss, az_recv.at[b], (row, dev_zl * 4 + y))
        pl.when(cond)(copy.start)
        conditional.append((cond, copy))

    def a_z_own(i):
        if i == 0:
            a_z_send(zl < 3, zl, mod4(zl + 1), az_own.at[0])
        else:
            a_z_send(zl > 0, zl, mod4(zl - 1), az_own.at[1])

    other = [
        jnp.where(zl == 0, 1, jnp.where(zl == 1, 0, jnp.where(zl == 2, 1, 2))),
        jnp.where(zl == 0, 2, jnp.where(zl == 1, 2, jnp.where(zl == 2, 3, 1))),
        jnp.where(zl == 0, 3, jnp.where(zl == 1, 3, 0)),
    ]

    def a_z_step(i):
        b = other[i]
        arrive(a_block(b, y), az_fwd.at[b], az_recv.at[b])
        from_left = b < zl
        dev_zl = jnp.where(from_left, zl + 1, zl - 1)
        a_z_send((dev_zl >= 0) & (dev_zl <= 3), b, mod4(dev_zl), az_fwd.at[b])
        a_y_start(b)

    offsets = (0, -1, 1, 2)

    def l_block(m, k, dx):
        leaf, off, width = CHUNKS[m]
        return l_buf[leaf].at[row_of(x + dx, zh + offsets[k], c), :, :, pl.ds(off, width)]

    def l_sib_block(m, k, dx):
        leaf, off, width = CHUNKS[m]
        return l_buf[leaf].at[row_of(x + dx, zh + offsets[k], 1 - c), :, :, pl.ds(off, width)]

    def l_relay(m, k, t):
        ref = l_block(m, k, offsets[t])
        send(ref, ref, lc_send.at[m, k, t], lc_recv.at[m, k, t], sib)

    def l_z_start(m):
        ref = l_block(m, 0, 0)
        for t, d in enumerate((1, -1)):
            send(ref, ref, lz_send.at[m, t], lz_recv.at[m, t], zh_dev[d])

    def l_z_start1(m, t):
        ref = l_block(m, 0, 0)
        send(ref, ref, lz_send.at[m, t], lz_recv.at[m, t], zh_dev[(1, -1)[t]])

    def l_z_forward1(m, t):
        ref = l_block(m, 1 + t, 0)
        arrive(ref, lz_send.at[m, t], lz_recv.at[m, t])
        half = ref.at[t]
        send(half, half, lz_send.at[m, 2 + t], lz_recv.at[m, 2 + t], zh_dev[(1, -1)[t]])
        l_x_start(m, 1 + t)

    def l_x_forward1(m, k, t):
        d = (1, -1)[t]
        ref = l_block(m, k, -d)
        arrive(ref, lx_send.at[m, k, t], lx_recv.at[m, k, t])
        half = ref.at[t]
        send(half, half, lx_send.at[m, k, 2 + t], lx_recv.at[m, k, 2 + t], x_dev[d])
        l_relay(m, k, 1 + t)

    def l_z_forward(m):
        for t, d in enumerate((1, -1)):
            ref = l_block(m, 1 + t, 0)
            arrive(ref, lz_send.at[m, t], lz_recv.at[m, t])
            half = ref.at[t]
            send(half, half, lz_send.at[m, 2 + t], lz_recv.at[m, 2 + t], zh_dev[d])
            l_x_start(m, 1 + t)

    def l_z_finish(m):
        for t in range(2):
            half = l_block(m, 3, 0).at[t]
            arrive(half, lz_send.at[m, 2 + t], lz_recv.at[m, 2 + t])
        l_x_start(m, 3)

    def l_x_start(m, k):
        ref = l_block(m, k, 0)
        for t, d in enumerate((1, -1)):
            send(ref, ref, lx_send.at[m, k, t], lx_recv.at[m, k, t], x_dev[d])
        l_relay(m, k, 0)

    def l_x_forward(m, k):
        for t, d in enumerate((1, -1)):
            ref = l_block(m, k, -d)
            arrive(ref, lx_send.at[m, k, t], lx_recv.at[m, k, t])
            half = ref.at[t]
            send(half, half, lx_send.at[m, k, 2 + t], lx_recv.at[m, k, 2 + t], x_dev[d])
            l_relay(m, k, 1 + t)

    def l_x_finish(m, k):
        for t in range(2):
            half = l_block(m, k, 2).at[t]
            arrive(half, lx_send.at[m, k, 2 + t], lx_recv.at[m, k, 2 + t])
        l_relay(m, k, 3)

    def l_sib_group(m, group):
        for k in (0, 1, 2) if group == 0 else (3,):
            for t in range(4):
                arrive(l_sib_block(m, k, offsets[t]), lc_send.at[m, k, t], lc_recv.at[m, k, t])

    def l_sib_group(m, group):
        for k in (0, 1, 2) if group == 0 else (3,):
            for t in range(4):
                arrive(l_sib_block(m, k, offsets[t]), lc_send.at[m, k, t], lc_recv.at[m, k, t])

    block_row = row // 2

    def leaf_state(m):
        count = counts_ref[m]
        place, live = jnp.int32(0), jnp.int32(0)
        for q in range(SLOTS):
            hit = ((rows_ref[m, q] == block_row) & (count > q)).astype(jnp.int32)
            place += hit * q
            live += hit
        return count, place, live

    def a_split(b):
        def one(t, carry):
            high, low = split(a_buf[b * 4 + t].reshape(B, B))
            a_hl[b * 4 + t, :B] = high
            a_hl[b * 4 + t, B:] = low
            return carry

        lax.fori_loop(0, 4, one, 0)

    def compute(m, group):
        count, place, live = leaf_state(m)
        parity = zh // 2 if group == 0 else 1 - zh // 2
        slots = [2 * i + parity for i in range(4)]
        left = jnp.concatenate([a_hl[rows_ref[m, q]] for q in slots], axis=1)
        for part in range(2):
            rights = [
                l_buf[m][pl.ds(q * 4, 4), part].reshape(B, B)
                * (count > q).astype(jnp.int32).astype(jnp.float32)
                for q in slots
            ]
            r_high, r_low = split(jnp.concatenate(rights, axis=0))
            both = dot(left, r_high)
            value = both[:B] + (both[B:] + dot(left[:B], r_low))
            if group == 0:
                acc[m, part] = value
            else:
                acc[m, part] += value
        if group == 1:
            keep = -(live.astype(jnp.float32))
            half = B // 2
            real = (acc[m, 0, :half] - acc[m, 1, half:]) * keep
            imag = (acc[m, 1, :half] + acc[m, 0, half:]) * keep
            sel_ref[0, :, pl.ds(m * B, B)] = real
            sel_ref[1, :, pl.ds(m * B, B)] = imag

    def diagonal(m):
        count, place, live = leaf_state(m)
        half = B // 2
        real = sel_ref[0, :, pl.ds(m * B, B)]
        imag = sel_ref[1, :, pl.ds(m * B, B)]
        low = l_buf[m][pl.ds(place * 4 + c * 2, 2)]
        low_real, low_imag = low[:, 0].reshape(half, B), low[:, 1].reshape(half, B)
        for part in range(2):
            if part == 0:
                left = jnp.concatenate([real, -imag], axis=0)
                right = jnp.concatenate([low_real, low_imag], axis=0)
            else:
                left = jnp.concatenate([real, imag], axis=0)
                right = jnp.concatenate([low_imag, low_real], axis=0)
            l_high, l_low = split(left)
            r_high, r_low = split(right)
            value = dot_t(l_high, r_high) + (dot_t(l_low, r_high) + dot_t(l_high, r_low))
            d_buf[m, :, :, part] = value.reshape(16, 2, 8, B)

    def rs0(m):
        send(d_buf.at[m, :, 1 - c], sib_buf.at[m], rs_send.at[m, 0], rs_recv.at[m, 0], sib)

    def rs1(m):
        arrive(sib_buf.at[m], rs_send.at[m, 0], rs_recv.at[m, 0])
        c_buf[m] = (d_buf[m, :, c] + sib_buf[m]).reshape(4, 4, 2, 8, B)
        for t, d in enumerate((1, -1)):
            send(
                c_buf.at[m, mod4(x + 2), :, t],
                x1_buf.at[m, t],
                rs_send.at[m, 1 + t],
                rs_recv.at[m, 1 + t],
                x_dev[d],
            )

    def rs2(m):
        for t, d in enumerate((1, -1)):
            arrive(x1_buf.at[m, t], rs_send.at[m, 1 + t], rs_recv.at[m, 1 + t])
            place = mod4(x + d)
            c_buf[m, place, :, t] = c_buf[m, place, :, t] + x1_buf[m, t]
            send(
                c_buf.at[m, place],
                x2_buf.at[m, t],
                rs_send.at[m, 3 + t],
                rs_recv.at[m, 3 + t],
                x_dev[d],
            )

    def rs3(m):
        for t in range(2):
            arrive(x2_buf.at[m, t], rs_send.at[m, 3 + t], rs_recv.at[m, 3 + t])
        e_buf[m] = c_buf[m, x] + (x2_buf[m, 0] + x2_buf[m, 1])
        for t, d in enumerate((1, -1)):
            send(
                e_buf.at[m, mod4(zh + 2), t],
                z1_buf.at[m, t],
                rs_send.at[m, 5 + t],
                rs_recv.at[m, 5 + t],
                zh_dev[d],
            )

    def rs4(m):
        for t, d in enumerate((1, -1)):
            arrive(z1_buf.at[m, t], rs_send.at[m, 5 + t], rs_recv.at[m, 5 + t])
            place = mod4(zh + d)
            e_buf[m, place, t] = e_buf[m, place, t] + z1_buf[m, t]
            send(
                e_buf.at[m, place],
                z2_buf.at[m, t],
                rs_send.at[m, 7 + t],
                rs_recv.at[m, 7 + t],
                zh_dev[d],
            )

    def rs5(m):
        for t in range(2):
            arrive(z2_buf.at[m, t], rs_send.at[m, 7 + t], rs_recv.at[m, 7 + t])
        total = e_buf[m, zh] + (z2_buf[m, 0] + z2_buf[m, 1])
        out_ref[:, :, pl.ds(m * B, B)] = diag_ref[:, :, pl.ds(m * B, B)] - total

    l_x_start(1,0)
    a_z_own(0)
    l_z_start1(0,0)
    l_z_start1(1,0)
    l_x_start(2,0)
    a_z_own(1)
    l_x_start(0,0)
    l_z_start1(1,1)
    l_z_start1(0,1)
    a_z_step(0)
    a_y_start(zl)
    a_z_step(1)
    l_z_forward1(0,0)
    l_z_forward1(1,0)
    l_z_forward1(0,1)
    l_x_forward1(0,2,1)
    l_x_forward1(2,0,0)
    l_z_start1(2,1)
    l_x_forward1(0,0,1)
    l_x_forward1(1,0,1)
    a_y_forward1(other[0],0)
    l_x_forward1(1,0,0)
    a_y_forward1(other[1],1)
    a_y_forward1(other[0],1)
    l_x_forward1(2,0,1)
    l_x_forward1(0,1,0)
    a_y_forward1(zl,1)
    l_x_forward1(0,2,0)
    l_x_forward1(1,1,1)
    l_z_start1(2,0)
    l_x_forward1(0,0,0)
    a_y_forward1(other[1],0)
    l_z_forward1(1,1)
    a_y_forward1(zl,0)
    l_z_finish(0)
    l_x_forward1(0,1,1)
    a_y_finish(other[0])
    l_x_finish(0,2)
    a_z_step(2)
    l_z_forward1(2,1)
    l_z_finish(1)
    l_x_forward1(1,2,1)
    a_y_finish(other[1])
    l_x_finish(0,1)
    l_x_forward1(1,1,0)
    l_z_forward1(2,0)
    l_x_forward1(1,2,0)
    l_x_finish(1,0)
    l_x_finish(0,0)
    l_z_finish(2)
    l_x_forward1(0,3,1)
    a_split(other[0])
    l_x_forward1(0,3,0)
    l_x_forward1(2,1,1)
    a_y_forward1(other[2],0)
    l_x_finish(1,2)
    a_y_forward1(other[2],1)
    l_x_forward1(2,2,1)
    l_x_finish(2,0)
    a_split(other[1])
    a_y_finish(zl)
    l_sib_group(0,0)
    l_x_forward1(2,1,0)
    l_x_finish(1,1)
    l_x_forward1(2,2,0)
    l_sib_group(1,0)
    l_x_finish(2,1)
    l_x_finish(0,3)
    l_x_finish(2,2)
    l_x_forward1(1,3,0)
    a_y_finish(other[2])
    l_x_forward1(2,3,1)
    l_x_forward1(1,3,1)
    a_split(other[2])
    a_split(zl)
    compute(0,0)
    l_x_forward1(2,3,0)
    l_sib_group(0,1)
    l_sib_group(2,0)
    compute(1,0)
    compute(0,1)
    l_x_finish(1,3)
    l_x_finish(2,3)
    diagonal(0)
    l_sib_group(1,1)
    rs0(0)
    l_sib_group(2,1)
    compute(1,1)
    diagonal(1)
    rs0(1)
    rs1(0)
    rs1(1)
    rs2(0)
    rs2(1)
    rs3(0)
    rs3(1)
    rs4(0)
    rs4(1)
    rs5(1)
    rs5(0)
    for copy in sent:
        copy.wait_send()
    for cond, copy in conditional:
        pl.when(cond)(copy.wait_send)


def on_device(top_inverse, panel, leaf_rows, leaf_counts, diag_inverse):
    f32 = jnp.float32
    any_space = pl.BlockSpec(memory_space=pl.ANY)
    vmem = pl.BlockSpec(memory_space=pltpu.VMEM)
    smem = pl.BlockSpec(memory_space=pltpu.SMEM)
    dma = pltpu.SemaphoreType.DMA
    return pl.pallas_call(
        kernel,
        out_shape=(
            pltpu.VMEM((2, B // 2, LEAVES * B), f32),
            pltpu.VMEM((2, 8, LEAVES * B), f32),
        ),
        in_specs=[smem, smem, any_space, any_space, vmem],
        out_specs=(vmem, vmem),
        scratch_shapes=[
            pltpu.VMEM((16, 2, B // 2, B), f32),
            pltpu.VMEM((32, 2, 64, B), f32),
            pltpu.VMEM((32, 2, 64, B), f32),
            pltpu.VMEM((16, 2 * B, B), jnp.bfloat16),
            pltpu.VMEM((LEAVES, 2, B, B), f32),
            pltpu.VMEM((LEAVES, 16, 2, 2, 8, B), f32),
            pltpu.VMEM((LEAVES, 16, 2, 8, B), f32),
            pltpu.VMEM((LEAVES, 4, 4, 2, 8, B), f32),
            pltpu.VMEM((LEAVES, 2, 4, 8, B), f32),
            pltpu.VMEM((LEAVES, 2, 4, 2, 8, B), f32),
            pltpu.VMEM((LEAVES, 4, 2, 8, B), f32),
            pltpu.VMEM((LEAVES, 2, 8, B), f32),
            pltpu.VMEM((LEAVES, 2, 2, 8, B), f32),
            dma((3,)),
            dma((2,)),
            dma((4,)),
            dma((4,)),
            dma((4, 4)),
            dma((4, 4)),
            dma((NC, 4)),
            dma((NC, 4)),
            dma((NC, 4, 4)),
            dma((NC, 4, 4)),
            dma((NC, 4, 4)),
            dma((NC, 4, 4)),
            dma((LEAVES, 9)),
            dma((LEAVES, 9)),
        ],
        compiler_params=pltpu.CompilerParams(collective_id=0, has_side_effects=True),
    )(leaf_rows, leaf_counts, top_inverse, panel, diag_inverse)


def solution(mesh):
    return jax.shard_map(
        on_device,
        mesh=mesh,
        in_specs=(
            P(None, "row", "col"),
            P(None, "row", "col"),
            P("col", None),
            P("col"),
            P(None, "row", "col"),
        ),
        out_specs=(P(None, "row", "col"), P(None, "row", "col")),
        check_vma=False,
    )
```

```python
import jax
import jax.numpy as jnp
from jax import lax
from jax.experimental import pallas as pl
from jax.experimental.pallas import tpu as pltpu
from jax.sharding import PartitionSpec as P

MESH = pl.DeviceIdType.MESH
B = 256
SLOTS = 8
LEAVES = 2
CHUNKS = ((0, 0, 256), (1, 0, 256))
NC = len(CHUNKS)


def split(value):
    high = value.astype(jnp.bfloat16)
    low = (value - high.astype(jnp.float32)).astype(jnp.bfloat16)
    return high, low


def dot(left, right):
    return jnp.dot(left, right, preferred_element_type=jnp.float32)


def dot_t(left, right):
    return lax.dot_general(
        left, right, (((0,), (0,)), ((), ())), preferred_element_type=jnp.float32
    )


def kernel(
    rows_ref,
    counts_ref,
    top_ref,
    panel_ref,
    diag_ref,
    sel_ref,
    out_ref,
    a_buf,
    l_buf0,
    l_buf1,
    a_hl,
    acc,
    d_buf,
    sib_buf,
    c_buf,
    x1_buf,
    x2_buf,
    e_buf,
    z1_buf,
    z2_buf,
    local_sem,
    az_own,
    az_fwd,
    az_recv,
    ay_send,
    ay_recv,
    lz_send,
    lz_recv,
    lx_send,
    lx_recv,
    lc_send,
    lc_recv,
    rs_send,
    rs_recv,
):
    l_buf = (l_buf0, l_buf1)
    row = lax.axis_index("row")
    col = lax.axis_index("col")
    x, zh, c = row // 8, (row // 2) % 4, row % 2
    zl, y = col // 4, col % 4

    def mod4(v):
        return (v + 8) % 4

    def row_of(xx, zz, cc):
        return (mod4(xx) * 4 + mod4(zz)) * 2 + cc

    sib = (row_of(x, zh, 1 - c), col)
    x_dev = {d: (row_of(x + d, zh, c), col) for d in (-1, 1)}
    zh_dev = {d: (row_of(x, zh + d, c), col) for d in (-1, 1)}
    y_dev = {d: (row, zl * 4 + mod4(y + d)) for d in (-1, 1)}

    own = [
        pltpu.make_async_copy(top_ref, a_buf.at[col], local_sem.at[0]),
    ] + [
        pltpu.make_async_copy(
            panel_ref.at[:, :, pl.ds(m * B, B)], l_buf[m].at[row], local_sem.at[1 + m]
        )
        for m in range(LEAVES)
    ]
    for copy in own:
        copy.start()

    barrier = pltpu.get_barrier_semaphore()
    greet = [sib, x_dev[-1], x_dev[1], zh_dev[-1], zh_dev[1], y_dev[-1], y_dev[1]]
    greet += [(row, mod4(zl + d) * 4 + y) for d in (-1, 1)]
    for dev in greet:
        pl.semaphore_signal(barrier, inc=1, device_id=dev, device_id_type=MESH)
    pl.semaphore_wait(barrier, len(greet))
    for copy in own:
        copy.wait()

    sent = []

    def desc(src, dst, ss, rs, dev):
        return pltpu.make_async_remote_copy(
            src_ref=src,
            dst_ref=dst,
            send_sem=ss,
            recv_sem=rs,
            device_id=dev,
            device_id_type=MESH,
        )

    def send(src, dst, ss, rs, dev):
        copy = desc(src, dst, ss, rs, dev)
        copy.start()
        sent.append(copy)

    def arrive(dst, ss, rs):
        desc(dst, dst, ss, rs, sib).wait_recv()

    def a_block(b, yy):
        return a_buf.at[b * 4 + mod4(yy)]

    def a_y_start(b):
        for t, d in enumerate((1, -1)):
            ref = a_block(b, y)
            send(ref, ref, ay_send.at[b, t], ay_recv.at[b, t], y_dev[d])

    def a_y_forward(b):
        for t, d in enumerate((1, -1)):
            ref = a_block(b, y - d)
            arrive(ref, ay_send.at[b, t], ay_recv.at[b, t])
            half = ref.at[t]
            send(half, half, ay_send.at[b, 2 + t], ay_recv.at[b, 2 + t], y_dev[d])

    def a_y_forward1(b, t):
        d = (1, -1)[t]
        ref = a_block(b, y - d)
        arrive(ref, ay_send.at[b, t], ay_recv.at[b, t])
        half = ref.at[t]
        send(half, half, ay_send.at[b, 2 + t], ay_recv.at[b, 2 + t], y_dev[d])

    def a_y_finish(b):
        for t in range(2):
            half = a_block(b, y + 2).at[t]
            arrive(half, ay_send.at[b, 2 + t], ay_recv.at[b, 2 + t])

    conditional = []

    def a_z_send(cond, b, dev_zl, ss):
        ref = a_block(b, y)
        copy = desc(ref, ref, ss, az_recv.at[b], (row, dev_zl * 4 + y))
        pl.when(cond)(copy.start)
        conditional.append((cond, copy))

    def a_z_own(i):
        if i == 0:
            a_z_send(zl < 3, zl, mod4(zl + 1), az_own.at[0])
        else:
            a_z_send(zl > 0, zl, mod4(zl - 1), az_own.at[1])

    other = [
        jnp.where(zl == 0, 1, jnp.where(zl == 1, 0, jnp.where(zl == 2, 1, 2))),
        jnp.where(zl == 0, 2, jnp.where(zl == 1, 2, jnp.where(zl == 2, 3, 1))),
        jnp.where(zl == 0, 3, jnp.where(zl == 1, 3, 0)),
    ]

    def a_z_step(i):
        b = other[i]
        arrive(a_block(b, y), az_fwd.at[b], az_recv.at[b])
        from_left = b < zl
        dev_zl = jnp.where(from_left, zl + 1, zl - 1)
        a_z_send((dev_zl >= 0) & (dev_zl <= 3), b, mod4(dev_zl), az_fwd.at[b])
        a_y_start(b)

    offsets = (0, -1, 1, 2)

    def l_block(m, k, dx):
        leaf, off, width = CHUNKS[m]
        return l_buf[leaf].at[row_of(x + dx, zh + offsets[k], c), :, :, pl.ds(off, width)]

    def l_sib_block(m, k, dx):
        leaf, off, width = CHUNKS[m]
        return l_buf[leaf].at[row_of(x + dx, zh + offsets[k], 1 - c), :, :, pl.ds(off, width)]

    def l_relay(m, k, t):
        ref = l_block(m, k, offsets[t])
        send(ref, ref, lc_send.at[m, k, t], lc_recv.at[m, k, t], sib)

    def l_z_start(m):
        ref = l_block(m, 0, 0)
        for t, d in enumerate((1, -1)):
            send(ref, ref, lz_send.at[m, t], lz_recv.at[m, t], zh_dev[d])

    def l_z_start1(m, t):
        ref = l_block(m, 0, 0)
        send(ref, ref, lz_send.at[m, t], lz_recv.at[m, t], zh_dev[(1, -1)[t]])

    def l_z_forward1(m, t):
        ref = l_block(m, 1 + t, 0)
        arrive(ref, lz_send.at[m, t], lz_recv.at[m, t])
        half = ref.at[t]
        send(half, half, lz_send.at[m, 2 + t], lz_recv.at[m, 2 + t], zh_dev[(1, -1)[t]])
        l_x_start(m, 1 + t)

    def l_x_forward1(m, k, t):
        d = (1, -1)[t]
        ref = l_block(m, k, -d)
        arrive(ref, lx_send.at[m, k, t], lx_recv.at[m, k, t])
        half = ref.at[t]
        send(half, half, lx_send.at[m, k, 2 + t], lx_recv.at[m, k, 2 + t], x_dev[d])
        l_relay(m, k, 1 + t)

    def l_z_forward(m):
        for t, d in enumerate((1, -1)):
            ref = l_block(m, 1 + t, 0)
            arrive(ref, lz_send.at[m, t], lz_recv.at[m, t])
            half = ref.at[t]
            send(half, half, lz_send.at[m, 2 + t], lz_recv.at[m, 2 + t], zh_dev[d])
            l_x_start(m, 1 + t)

    def l_z_finish(m):
        for t in range(2):
            half = l_block(m, 3, 0).at[t]
            arrive(half, lz_send.at[m, 2 + t], lz_recv.at[m, 2 + t])
        l_x_start(m, 3)

    def l_x_start(m, k):
        ref = l_block(m, k, 0)
        for t, d in enumerate((1, -1)):
            send(ref, ref, lx_send.at[m, k, t], lx_recv.at[m, k, t], x_dev[d])
        l_relay(m, k, 0)

    def l_x_forward(m, k):
        for t, d in enumerate((1, -1)):
            ref = l_block(m, k, -d)
            arrive(ref, lx_send.at[m, k, t], lx_recv.at[m, k, t])
            half = ref.at[t]
            send(half, half, lx_send.at[m, k, 2 + t], lx_recv.at[m, k, 2 + t], x_dev[d])
            l_relay(m, k, 1 + t)

    def l_x_finish(m, k):
        for t in range(2):
            half = l_block(m, k, 2).at[t]
            arrive(half, lx_send.at[m, k, 2 + t], lx_recv.at[m, k, 2 + t])
        l_relay(m, k, 3)

    def l_sib_group(m, group):
        for k in (0, 1, 2) if group == 0 else (3,):
            for t in range(4):
                arrive(l_sib_block(m, k, offsets[t]), lc_send.at[m, k, t], lc_recv.at[m, k, t])

    def l_sib_group(m, group):
        for k in (0, 1, 2) if group == 0 else (3,):
            for t in range(4):
                arrive(l_sib_block(m, k, offsets[t]), lc_send.at[m, k, t], lc_recv.at[m, k, t])

    block_row = row // 2

    def leaf_state(m):
        count = counts_ref[m]
        place, live = jnp.int32(0), jnp.int32(0)
        for q in range(SLOTS):
            hit = ((rows_ref[m, q] == block_row) & (count > q)).astype(jnp.int32)
            place += hit * q
            live += hit
        return count, place, live

    def a_split(b):
        def one(t, carry):
            high, low = split(a_buf[b * 4 + t].reshape(B, B))
            a_hl[b * 4 + t, :B] = high
            a_hl[b * 4 + t, B:] = low
            return carry

        lax.fori_loop(0, 4, one, 0)

    def compute(m, group):
        count, place, live = leaf_state(m)
        parity = zh // 2 if group == 0 else 1 - zh // 2
        slots = [2 * i + parity for i in range(4)]
        left = jnp.concatenate([a_hl[rows_ref[m, q]] for q in slots], axis=1)
        for part in range(2):
            rights = [
                l_buf[m][pl.ds(q * 4, 4), part].reshape(B, B)
                * (count > q).astype(jnp.int32).astype(jnp.float32)
                for q in slots
            ]
            r_high, r_low = split(jnp.concatenate(rights, axis=0))
            both = dot(left, r_high)
            value = both[:B] + (both[B:] + dot(left[:B], r_low))
            if group == 0:
                acc[m, part] = value
            else:
                acc[m, part] += value
        if group == 1:
            keep = -(live.astype(jnp.float32))
            half = B // 2
            real = (acc[m, 0, :half] - acc[m, 1, half:]) * keep
            imag = (acc[m, 1, :half] + acc[m, 0, half:]) * keep
            sel_ref[0, :, pl.ds(m * B, B)] = real
            sel_ref[1, :, pl.ds(m * B, B)] = imag

    def diagonal(m):
        count, place, live = leaf_state(m)
        half = B // 2
        real = sel_ref[0, :, pl.ds(m * B, B)]
        imag = sel_ref[1, :, pl.ds(m * B, B)]
        low = l_buf[m][pl.ds(place * 4 + c * 2, 2)]
        low_real, low_imag = low[:, 0].reshape(half, B), low[:, 1].reshape(half, B)
        for part in range(2):
            if part == 0:
                left = jnp.concatenate([real, -imag], axis=0)
                right = jnp.concatenate([low_real, low_imag], axis=0)
            else:
                left = jnp.concatenate([real, imag], axis=0)
                right = jnp.concatenate([low_imag, low_real], axis=0)
            l_high, l_low = split(left)
            r_high, r_low = split(right)
            value = dot_t(l_high, r_high) + (dot_t(l_low, r_high) + dot_t(l_high, r_low))
            d_buf[m, :, :, part] = value.reshape(16, 2, 8, B)

    def rs0(m):
        send(d_buf.at[m, :, 1 - c], sib_buf.at[m], rs_send.at[m, 0], rs_recv.at[m, 0], sib)

    def rs1(m):
        arrive(sib_buf.at[m], rs_send.at[m, 0], rs_recv.at[m, 0])
        c_buf[m] = (d_buf[m, :, c] + sib_buf[m]).reshape(4, 4, 2, 8, B)
        for t, d in enumerate((1, -1)):
            send(
                c_buf.at[m, mod4(x + 2), :, t],
                x1_buf.at[m, t],
                rs_send.at[m, 1 + t],
                rs_recv.at[m, 1 + t],
                x_dev[d],
            )

    def rs2(m):
        for t, d in enumerate((1, -1)):
            arrive(x1_buf.at[m, t], rs_send.at[m, 1 + t], rs_recv.at[m, 1 + t])
            place = mod4(x + d)
            c_buf[m, place, :, t] = c_buf[m, place, :, t] + x1_buf[m, t]
            send(
                c_buf.at[m, place],
                x2_buf.at[m, t],
                rs_send.at[m, 3 + t],
                rs_recv.at[m, 3 + t],
                x_dev[d],
            )

    def rs3(m):
        for t in range(2):
            arrive(x2_buf.at[m, t], rs_send.at[m, 3 + t], rs_recv.at[m, 3 + t])
        e_buf[m] = c_buf[m, x] + (x2_buf[m, 0] + x2_buf[m, 1])
        for t, d in enumerate((1, -1)):
            send(
                e_buf.at[m, mod4(zh + 2), t],
                z1_buf.at[m, t],
                rs_send.at[m, 5 + t],
                rs_recv.at[m, 5 + t],
                zh_dev[d],
            )

    def rs4(m):
        for t, d in enumerate((1, -1)):
            arrive(z1_buf.at[m, t], rs_send.at[m, 5 + t], rs_recv.at[m, 5 + t])
            place = mod4(zh + d)
            e_buf[m, place, t] = e_buf[m, place, t] + z1_buf[m, t]
            send(
                e_buf.at[m, place],
                z2_buf.at[m, t],
                rs_send.at[m, 7 + t],
                rs_recv.at[m, 7 + t],
                zh_dev[d],
            )

    def rs5(m):
        for t in range(2):
            arrive(z2_buf.at[m, t], rs_send.at[m, 7 + t], rs_recv.at[m, 7 + t])
        total = e_buf[m, zh] + (z2_buf[m, 0] + z2_buf[m, 1])
        out_ref[:, :, pl.ds(m * B, B)] = diag_ref[:, :, pl.ds(m * B, B)] - total

    a_z_own(0)
    l_x_start(1,0)
    l_z_start1(0,0)
    l_z_start1(0,1)
    l_x_start(0,0)
    l_x_forward1(0,0,1)
    a_z_own(1)
    a_y_start(zl)
    a_z_step(0)
    l_z_forward1(0,1)
    a_z_step(1)
    l_z_forward1(0,0)
    l_x_forward1(0,2,0)
    a_y_forward1(other[1],0)
    a_y_forward1(other[0],0)
    a_y_forward1(other[1],1)
    a_y_forward1(zl,0)
    l_x_forward1(0,1,0)
    l_x_forward1(0,0,0)
    l_z_start1(1,1)
    l_z_start1(1,0)
    a_y_forward1(zl,1)
    l_x_forward1(0,2,1)
    l_x_finish(0,2)
    l_z_finish(0)
    l_x_forward1(0,1,1)
    a_y_finish(other[1])
    a_y_forward1(other[0],1)
    a_z_step(2)
    l_z_forward1(1,1)
    l_x_forward1(1,0,1)
    l_z_forward1(1,0)
    l_x_finish(0,0)
    a_y_finish(zl)
    l_x_forward1(0,3,1)
    l_x_forward1(1,0,0)
    l_x_forward1(0,3,0)
    a_y_forward1(other[2],0)
    a_y_finish(other[0])
    a_y_forward1(other[2],1)
    l_x_forward1(1,2,1)
    l_x_forward1(1,2,0)
    l_x_finish(1,0)
    a_split(other[1])
    l_x_finish(0,3)
    l_z_finish(1)
    a_split(zl)
    l_x_finish(0,1)
    a_split(other[0])
    l_x_forward1(1,1,1)
    a_y_finish(other[2])
    l_sib_group(0,1)
    l_sib_group(0,0)
    l_x_forward1(1,1,0)
    l_x_finish(1,2)
    a_split(other[2])
    compute(0,0)
    l_x_forward1(1,3,0)
    l_x_forward1(1,3,1)
    compute(0,1)
    l_x_finish(1,1)
    diagonal(0)
    l_x_finish(1,3)
    rs0(0)
    l_sib_group(1,0)
    compute(1,0)
    l_sib_group(1,1)
    compute(1,1)
    diagonal(1)
    rs0(1)
    rs1(0)
    rs1(1)
    rs2(0)
    rs2(1)
    rs3(0)
    rs3(1)
    rs4(0)
    rs4(1)
    rs5(1)
    rs5(0)
    for copy in sent:
        copy.wait_send()
    for cond, copy in conditional:
        pl.when(cond)(copy.wait_send)


def on_device(top_inverse, panel, leaf_rows, leaf_counts, diag_inverse):
    f32 = jnp.float32
    any_space = pl.BlockSpec(memory_space=pl.ANY)
    vmem = pl.BlockSpec(memory_space=pltpu.VMEM)
    smem = pl.BlockSpec(memory_space=pltpu.SMEM)
    dma = pltpu.SemaphoreType.DMA
    return pl.pallas_call(
        kernel,
        out_shape=(
            pltpu.VMEM((2, B // 2, LEAVES * B), f32),
            pltpu.VMEM((2, 8, LEAVES * B), f32),
        ),
        in_specs=[smem, smem, any_space, any_space, vmem],
        out_specs=(vmem, vmem),
        scratch_shapes=[
            pltpu.VMEM((16, 2, B // 2, B), f32),
            pltpu.VMEM((32, 2, 64, B), f32),
            pltpu.VMEM((32, 2, 64, B), f32),
            pltpu.VMEM((16, 2 * B, B), jnp.bfloat16),
            pltpu.VMEM((LEAVES, 2, B, B), f32),
            pltpu.VMEM((LEAVES, 16, 2, 2, 8, B), f32),
            pltpu.VMEM((LEAVES, 16, 2, 8, B), f32),
            pltpu.VMEM((LEAVES, 4, 4, 2, 8, B), f32),
            pltpu.VMEM((LEAVES, 2, 4, 8, B), f32),
            pltpu.VMEM((LEAVES, 2, 4, 2, 8, B), f32),
            pltpu.VMEM((LEAVES, 4, 2, 8, B), f32),
            pltpu.VMEM((LEAVES, 2, 8, B), f32),
            pltpu.VMEM((LEAVES, 2, 2, 8, B), f32),
            dma((3,)),
            dma((2,)),
            dma((4,)),
            dma((4,)),
            dma((4, 4)),
            dma((4, 4)),
            dma((NC, 4)),
            dma((NC, 4)),
            dma((NC, 4, 4)),
            dma((NC, 4, 4)),
            dma((NC, 4, 4)),
            dma((NC, 4, 4)),
            dma((LEAVES, 9)),
            dma((LEAVES, 9)),
        ],
        compiler_params=pltpu.CompilerParams(collective_id=0, has_side_effects=True),
    )(leaf_rows, leaf_counts, top_inverse, panel, diag_inverse)


def solution(mesh):
    return jax.shard_map(
        on_device,
        mesh=mesh,
        in_specs=(
            P(None, "row", "col"),
            P(None, "row", "col"),
            P("col", None),
            P("col"),
            P(None, "row", "col"),
        ),
        out_specs=(P(None, "row", "col"), P(None, "row", "col")),
        check_vma=False,
    )
```
